128 devices in a mesh: leaf: 32 (over z, y, core), row: 4 (over x).
Axes of the slice: x: 4, y: 4, z: 4, core: 2. Of those that a mesh axis runs over, the one named last changes fastest.
Arguments:
- lower: float32 [1, 4, 32, 4, 256, 512], P(None, None, 'leaf', 'row'), may hold values from -0.0625 to 0.0625
- inverse_diag: float32 [1, 5, 32, 4, 64, 512], P(None, None, 'leaf', 'row'), as said below
- structure: int32 [4, 16, 16], replicated, may hold values 0 or 1
Outputs:
- sigma_off: float32 [1, 4, 32, 4, 256, 512], P(None, None, 'leaf', 'row')
- sigma_diag: float32 [1, 5, 32, 4, 64, 512], P(None, None, 'leaf', 'row')
The draws below stay inside these ranges and needn't reach their ends.
Inputs may be any that keep to these rules, and one draw needn't show every extreme that they name: For each node, the block built from inverse_diag is lower triangular with a positive diagonal; unused row slots are zero. A 1 marks a tile of 128 ancestor rows in the node's structure; entries past a level's nodes or tiles are unused.
All inputs are finite; a program needn't handle non-finite values.
Results may differ from the reference program's by a relative error of at most 0.00017.
Values sent between devices are 32-bit elements; how exact they have to be, the bound alone decides.
No kernel may reach another device: no remote copies, remote signals or barrier semaphores. Data moves between devices by JAX's collectives and lax.ppermute only.
A program may use at most 128 MiB of HBM per device.

```python
import math
import jax
import jax.numpy as jnp
from jax import lax

W = 512
TILE = 128
H = 1
LEVELS = 5
NODEMAX = 16
PR = 256
DR = 64
MT = 16
N_LEAF = 32
N_ROW = 4


def draw_inverse_diag(key, part):
    pieces = []
    for tree_level in range(LEVELS):
        node_count = 2 ** tree_level
        level_key = jax.random.fold_in(key, 101 + tree_level)
        key_diag, key_low = jax.random.split(level_key)
        diagonal = jax.random.uniform(key_diag, (H, node_count, W), jnp.float32, 0.7, 1.3)
        lower_part = jax.random.normal(key_low, (H, node_count, W, W), jnp.float32) * (0.5 / math.sqrt(W))
        strict = jnp.tril(lower_part, -1)
        blocks = strict + diagonal[..., None] * jnp.eye(W, dtype=jnp.float32)
        diag_rows = W * node_count // (N_LEAF * N_ROW)
        shaped = blocks.reshape(H, N_LEAF, N_ROW, diag_rows, W)
        pieces.append(jnp.pad(shaped, ((0, 0), (0, 0), (0, 0), (0, DR - diag_rows), (0, 0))))
    return jnp.stack(pieces, 1)


def touch_ends(drawn, key, low, largest):
    longest = drawn.shape.index(max(drawn.shape))
    spots = []
    for shift in (0, 1):
        where = [jax.random.randint(jax.random.fold_in(key, axis), (), 0, length) for axis, length in enumerate(drawn.shape)]
        where[longest] = (where[longest] + shift) % drawn.shape[longest]
        spots.append(tuple(where))
    return drawn.at[spots[0]].set(low).at[spots[1]].set(largest)


def levels(rng, extent, cuts, low, top_value):
    level, own = 1.0, jax.random.fold_in(rng, 6)
    for dim, parts in cuts:
        heights = jnp.exp(jax.random.uniform(jax.random.fold_in(own, dim), (parts,), jnp.float32, low / len(cuts), top_value / len(cuts)))
        level = level * jnp.repeat(heights, extent[dim] // parts).reshape([-1 if axis == dim else 1 for axis in range(len(extent))])
    return level


def bell_draw(stream_key, extent, spread, bound, cuts=(), held_as=jnp.bfloat16):
    entries = spread * jax.random.normal(stream_key, extent, jnp.float32)
    if cuts:
        entries = entries * levels(stream_key, extent, cuts, -0.22, 0.18)
    return jnp.clip(entries, -bound, bound).astype(held_as)


def setup_inputs(seed: int = 0) -> dict:
    arg_keys = jax.random.split(jax.random.key(seed), 4)
    lower = bell_draw(arg_keys[0], (H, LEVELS - 1, N_LEAF, N_ROW, PR, W), (16 * W) ** -0.5, 0.0625, ((2, 32), (3, 4)), jnp.float32)
    inverse_diag = draw_inverse_diag(jax.random.fold_in(arg_keys[3], 71), 0)
    structure = touch_ends((jax.random.randint(arg_keys[2], (LEVELS - 1, NODEMAX, MT), 0, 4) < 3).astype(jnp.int32), jax.random.fold_in(arg_keys[2], 1), 0, 1)
    return {"lower": lower, "inverse_diag": inverse_diag, "structure": structure}


def node_rows(stacked, slot_level, first_leaf, group_size, row_count):
    shard_piece = stacked[:, slot_level, first_leaf:first_leaf + group_size, :, :row_count, :]
    return shard_piece.reshape(shard_piece.shape[0], group_size * shard_piece.shape[2] * row_count, shard_piece.shape[-1])


def reference(lower, inverse_diag, structure):
    settings = lower.shape[0]
    panel_width = inverse_diag.shape[-1]
    leaves = inverse_diag.shape[2]
    rowdev = inverse_diag.shape[3]
    highest = lax.Precision.HIGHEST
    sigma_off = jnp.zeros(lower.shape, jnp.float32)
    sigma_diag = jnp.zeros(inverse_diag.shape, jnp.float32)
    ancestor_blocks = {}
    for tree_level in range(LEVELS):
        group_size = leaves >> tree_level
        diag_rows = panel_width * 2 ** tree_level // (leaves * rowdev)
        off_rows = tree_level * diag_rows
        for node_index in range(2 ** tree_level):
            first_leaf = node_index * group_size
            inverse_full = node_rows(inverse_diag, tree_level, first_leaf, group_size, diag_rows)
            base_term = jnp.einsum("hki,hkj->hij", inverse_full, inverse_full, precision=highest)
            if tree_level == 0:
                sigma_block = base_term
                child_block = sigma_block
            else:
                above = ancestor_blocks[(tree_level - 1, node_index // 2)]
                panel_full = node_rows(lower, tree_level - 1, first_leaf, group_size, off_rows)
                tile_flags = structure[tree_level - 1, node_index, :tree_level * panel_width // TILE]
                row_mask = jnp.repeat(tile_flags.astype(jnp.float32), TILE)
                panel_full = panel_full * row_mask[None, :, None]
                unit_panel = jnp.einsum("hrk,hkj->hrj", panel_full, inverse_full, precision=highest)
                sigma_cols = -jnp.einsum("hrs,hsj->hrj", above, unit_panel, precision=highest)
                sigma_block = base_term - jnp.einsum("hsi,hsj->hij", unit_panel, sigma_cols, precision=highest)
                upper_rows = jnp.concatenate([above, sigma_cols], 2)
                lower_rows = jnp.concatenate([jnp.swapaxes(sigma_cols, 1, 2), sigma_block], 2)
                child_block = jnp.concatenate([upper_rows, lower_rows], 1)
                sigma_off = sigma_off.at[:, tree_level - 1, first_leaf:first_leaf + group_size, :, :off_rows, :].set(
                    sigma_cols.reshape(settings, group_size, rowdev, off_rows, panel_width))
            if tree_level + 1 < LEVELS:
                ancestor_blocks[(tree_level, node_index)] = child_block
            sigma_diag = sigma_diag.at[:, tree_level, first_leaf:first_leaf + group_size, :, :diag_rows, :].set(
                sigma_block.reshape(settings, group_size, rowdev, diag_rows, panel_width))
    return sigma_off, sigma_diag
```

```python
import jax
import jax.numpy as jnp
from jax import lax
from jax.sharding import PartitionSpec as P

TILE = 128
HIGH = lax.Precision.HIGH


def mm(a, b):
    return jnp.dot(a, b, precision=HIGH)


def mtm(a, b):
    return lax.dot_general(a, b, (((0,), (0,)), ((), ())), precision=HIGH)


def swap(block, move):
    route = []
    for z in range(4):
        for y in range(4):
            for c in range(2):
                for x in range(4):
                    z2, y2, c2, x2 = move(z, y, c, x)
                    route.append((((z * 4 + y) * 2 + c) * 4 + x, ((z2 * 4 + y2) * 2 + c2) * 4 + x2))
    return lax.ppermute(block, ("leaf", "row"), route)


def over_x(bits):
    return lambda z, y, c, x: (z, y, c, x ^ bits)


def over_y(bits):
    return lambda z, y, c, x: (z, y ^ bits, c, x)


def over_z(bits):
    return lambda z, y, c, x: (z ^ bits, y, c, x)


def over_core(z, y, c, x):
    return (z, y, 1 - c, x)


def order2(bit, own, other):
    return jnp.where(bit == 1, jnp.stack([other, own]), jnp.stack([own, other]))


def order4(index, own, one, two, three):
    odd = index & 1 == 1
    a, b = jnp.where(odd, one, own), jnp.where(odd, own, one)
    c, d = jnp.where(odd, three, two), jnp.where(odd, two, three)
    return jnp.where(index & 2 == 2, jnp.stack([c, d, a, b]), jnp.stack([a, b, c, d]))


def gather_direct(own, index, over):
    one, two, three = (swap(own, over(bits)) for bits in (1, 2, 3))
    return order4(index, own, one, two, three)


def gather_ring(own, index, over):
    half = own.shape[0] // 2
    one, three = swap(own, over(1)), swap(own, over(3))
    two = jnp.concatenate([swap(one[:half], over(3)), swap(three[half:], over(1))], 0)
    return order4(index, own, one, two, three)


def on_device(lower, inverse_diag, structure):
    low = lower[0, :, 0, 0]
    dia = inverse_diag[0, :, 0, 0]
    width = dia.shape[-1]
    leaf = lax.axis_index("leaf")
    x = lax.axis_index("row")
    z, y, c = leaf >> 3, (leaf >> 1) & 3, leaf & 1

    def flags(level):
        node = leaf >> (5 - level)
        rows = lax.dynamic_index_in_dim(structure[level - 1], node, 0, keepdims=False)
        return jnp.repeat(rows[: level * width // TILE].astype(jnp.float32), TILE)[:, None]

    piece0, piece1 = dia[0, :4], jnp.concatenate([dia[1, :8], low[0, :8]], 0)
    one, two, three = swap(jnp.concatenate([piece1, piece0], 0), over_z(1)), swap(piece0, over_z(2)), swap(piece0, over_z(3))
    top = order4(z, piece0, one[16:], two, three).reshape(16, width)
    second = order2(z & 1, piece1, one[:16]).reshape(32, width)
    early = jnp.concatenate([second, top, dia[2, :16], low[1, :32]], 0)
    early = gather_direct(early, x, over_x)
    upper = gather_ring(early[:, :48].reshape(4 * 48, width).reshape(192, width), y, over_y)
    upper = upper.reshape(4, 4, 48, width)
    upper = order2(c, upper, swap(upper, over_core))
    mid = gather_ring(early[:, 48:].reshape(192, width), y, over_y).reshape(4, 4, 48, width)
    mid = order2(c, mid, swap(mid, over_core))
    level1 = upper[:, :, :, :32].reshape(2, 4, 4, 2, 16, width).transpose(3, 1, 0, 2, 4, 5)
    d1 = level1[..., :8, :].reshape(512, width)
    b1 = level1[..., 8:, :].reshape(512, width)
    d0 = upper[:, :, :, 32:].reshape(2, 4, 4, 4, 4, width).transpose(3, 1, 0, 2, 4, 5).reshape(512, width)
    mid = mid.transpose(1, 0, 2, 3, 4)
    d2 = mid[..., :16, :].reshape(512, width)
    b2 = mid[..., 16:, :].reshape(1024, width)

    d3 = order2(y & 1, dia[3, :32], swap(dia[3, :32], over_y(1))).reshape(64, width)
    third = gather_ring(jnp.concatenate([d3, low[2, :96]], 0), x, over_x)
    b3 = third[:, 64:].reshape(384, width)
    b3 = order2(y & 1, b3, swap(b3, over_y(1)))
    b3 = order2(c, b3, swap(b3, over_core)).reshape(2, 2, 384, width).transpose(1, 0, 2, 3).reshape(1536, width)
    d3 = third[:, :64]
    d3 = order2(c, d3, swap(d3, over_core)).reshape(2, 4, 2, 32, width).transpose(2, 0, 1, 3, 4).reshape(512, width)

    fourth = gather_ring(jnp.concatenate([dia[4, :64], low[3, :256]], 0), x, over_x)
    fourth = order2(c, fourth, swap(fourth, over_core))
    d4 = fourth[:, :, :64].reshape(512, width)
    b4 = fourth[:, :, 64:].reshape(2048, width)

    offs, diags = [], []

    def emit(parts, piece, slots):
        parts.append(jnp.pad(piece, ((0, slots - piece.shape[0]), (0, 0))))

    above = mtm(d0, d0)
    emit(diags, lax.dynamic_slice_in_dim(above, (leaf * 4 + x) * 4, 4, 0), 64)
    for level, d, b in ((1, d1, b1), (2, d2, b2)):
        unit = mm(b * flags(level), d)
        cols = -mm(above, unit)
        block = mtm(d, d) - mtm(unit, cols)
        place = (leaf % (32 >> level)) * 4 + x
        rows = 4 << level
        emit(offs, lax.dynamic_slice_in_dim(cols, place * rows * level, rows * level, 0), 256)
        emit(diags, lax.dynamic_slice_in_dim(block, place * rows, rows, 0), 64)
        above = jnp.concatenate(
            [jnp.concatenate([above, cols], 1), jnp.concatenate([cols.T, block], 1)], 0
        )

    place = (leaf % 4) * 4 + x
    unit3 = mm(b3 * flags(3), d3)
    emit(offs, -mm(lax.dynamic_slice_in_dim(above, place * 96, 96, 0), unit3), 256)
    unit_i = lax.dynamic_slice_in_dim(unit3, place * 32, 32, 1)
    d_i = lax.dynamic_slice_in_dim(d3, place * 32, 32, 1)
    emit(diags, mtm(d_i, d3) + mm(mtm(unit_i, above), unit3), 64)

    half = width // 2
    d_h = lax.dynamic_slice_in_dim(d4, c * half, half, 1)
    unit_h = mm(b4 * flags(4), d_h)
    upper_u, lower_u = unit_h[:1536], unit_h[1536:]
    rest = upper_u - mm(unit3, lower_u)
    top_c = -mm(above, rest)
    low_c = -mtm(unit3, top_c) - mtm(d3, mm(d3, lower_u))
    cols4 = jnp.concatenate([top_c, low_c], 0)
    mine = lax.dynamic_slice_in_dim(cols4, c * 1024 + x * 256, 256, 0)
    theirs = lax.dynamic_slice_in_dim(cols4, (1 - c) * 1024 + x * 256, 256, 0)
    got = swap(theirs, over_core)
    first = c == 0
    emit(offs, jnp.where(first, jnp.concatenate([mine, got], 1), jnp.concatenate([got, mine], 1)), 256)
    unit_i = lax.dynamic_slice_in_dim(unit_h, x * 64, 64, 1)
    unit_o = swap(unit_i, over_core)
    d_mine = lax.dynamic_slice_in_dim(d4, c * half + x * 64, 64, 1)
    d_other = lax.dynamic_slice_in_dim(d4, (1 - c) * half + x * 64, 64, 1)
    mine = mtm(d_mine, d_h) - mtm(unit_i, cols4)
    theirs = mtm(d_other, d_h) - mtm(unit_o, cols4)
    got = swap(theirs, over_core)
    emit(diags, jnp.where(first, jnp.concatenate([mine, got], 1), jnp.concatenate([got, mine], 1)), 64)
    sigma_off = jnp.stack(offs)[None, :, None, None]
    sigma_diag = jnp.stack(diags)[None, :, None, None]
    return (sigma_off, sigma_diag)


def solution(mesh):
    placed = P(None, None, "leaf", "row", None, None)
    return jax.shard_map(
        on_device,
        mesh=mesh,
        in_specs=(placed, placed, P()),
        out_specs=(placed, placed),
        check_vma=False,
    )
```

```python
import functools

import jax
import jax.numpy as jnp
from jax import lax
from jax.experimental import pallas as pl
from jax.experimental.pallas import tpu as pltpu
from jax.sharding import PartitionSpec as P

W = 512
F32 = jnp.float32
BF16 = jnp.bfloat16
VMEM = pl.BlockSpec(memory_space=pltpu.VMEM)
NN = (((1,), (0,)), ((), ()))
NT = (((1,), (1,)), ((), ()))


def swap(block, move):
    route = []
    for z in range(4):
        for y in range(4):
            for c in range(2):
                for x in range(4):
                    z2, y2, c2, x2 = move(z, y, c, x)
                    route.append((((z * 4 + y) * 2 + c) * 4 + x, ((z2 * 4 + y2) * 2 + c2) * 4 + x2))
    return lax.ppermute(block, ("leaf", "row"), route)


def over_x(bits):
    return lambda z, y, c, x: (z, y, c, x ^ bits)


def over_y(bits):
    return lambda z, y, c, x: (z, y ^ bits, c, x)


def over_z(bits):
    return lambda z, y, c, x: (z ^ bits, y, c, x)


def over_core(z, y, c, x):
    return (z, y, 1 - c, x)


def ring(own, over):
    half = own.shape[0] // 2
    one, three = swap(own, over(1)), swap(own, over(3))
    return [own, one, three, swap(one[:half], over(3)), swap(three[half:], over(1))]


def both_cores(parts):
    return parts + [swap(part, over_core) for part in parts]


def here():
    leaf = lax.axis_index("leaf")
    return leaf >> 3, (leaf >> 1) & 3, leaf & 1, lax.axis_index("row")


def split(value):
    high = value.astype(BF16)
    return high, (value - high.astype(F32)).astype(BF16)


def dot3(a, b, dims=NN):
    one = functools.partial(lax.dot_general, dimension_numbers=dims, preferred_element_type=F32)
    return one(a[0], b[0]) + (one(a[0], b[1]) + one(a[1], b[0]))


def pack_kernel(flags, low, dia, second, top, third, fourth, fifth, sems):
    z, y, c, x = here()
    leaf = (z * 4 + y) * 2 + c
    copies = []

    def copy(src, dst):
        copies.append(pltpu.make_async_copy(src, dst, sems.at[len(copies)]))
        copies[-1].start()

    copy(dia.at[0, 1, 0, 0, 0:8], second.at[0:8])
    copy(low.at[0, 0, 0, 0, 0:8], second.at[8:16])
    copy(dia.at[0, 0, 0, 0, 0:8], second.at[16:24])
    copy(dia.at[0, 0, 0, 0, 0:8], top)
    copy(dia.at[0, 2, 0, 0, 0:16], third.at[0:16])
    copy(low.at[0, 1, 0, 0, 0:32], third.at[16:48])
    copy(dia.at[0, 3, 0, 0, 0:32], fourth.at[0:32])
    copy(low.at[0, 2, 0, 0, 0:96], fourth.at[32:128])
    copy(dia.at[0, 4, 0, 0, 0:64], fifth.at[0:64])
    copy(low.at[0, 3, 0, 0, 0:256], fifth.at[64:320])
    for item in copies:
        item.wait()

    def keep(level, ref, start, count, step):
        group = 32 >> level
        place = (leaf % group) * 4 + x
        rows = level * (4 << level)
        for offset in range(0, count, step):
            flag = flags[level - 1, leaf // group, (place * rows + offset) // 128].astype(F32)
            span = pl.ds(start + offset, step)
            ref[span, :] = ref[span, :] * flag

    keep(1, second, 8, 8, 8)
    keep(2, third, 16, 32, 32)
    keep(3, fourth, 32, 96, 32)
    keep(4, fifth, 64, 256, 128)


def pack(structure, lower, inverse_diag):
    rows = (24, 8, 48, 128, 320)
    return pl.pallas_call(
        pack_kernel,
        out_shape=[jax.ShapeDtypeStruct((n, W), F32) for n in rows],
        in_specs=[pl.BlockSpec(memory_space=pltpu.SMEM), pl.BlockSpec(memory_space=pl.ANY), pl.BlockSpec(memory_space=pl.ANY)],
        out_specs=[VMEM] * len(rows),
        scratch_shapes=[pltpu.SemaphoreType.DMA((10,))],
        name="pack",
    )(structure, lower, inverse_diag)


def y_parts():
    return [(0, (0, 1, 2, 3)), (1, (0, 1, 2, 3)), (3, (0, 1, 2, 3)), (2, (0, 1)), (2, (2, 3))]


def upper_kernel(*refs):
    parts, refs = refs[:10], refs[10:]
    ah, al, s0, c1, s1, c2, s2, d0, d1, d2, b1, b2, dh, dl, uh, ul, vh, vl, ch, cl, cf = refs
    z, y, c, x = here()
    count = 0
    for number, (dy, xs) in enumerate(y_parts() * 2):
        core = c ^ (number // 5)
        for block, dx in enumerate(xs):
            source = parts[number]
            base = block * 96
            place = ((y ^ dy) * 2 + core) * 4 + (x ^ dx)
            d2[pl.ds(place * 16, 16), :] = source[base : base + 16, :]
            b2[pl.ds(place * 32, 32), :] = source[base + 16 : base + 48, :]
            for dz in range(2):
                at = pl.ds(((((z ^ dz) & 1) * 32) + place) * 8, 8)
                d1[at, :] = source[base + 48 + dz * 16 : base + 56 + dz * 16, :]
                b1[at, :] = source[base + 56 + dz * 16 : base + 64 + dz * 16, :]
            d0[count * 16 : count * 16 + 16, :] = source[base + 80 : base + 96, :]
            count += 1

    def put(rows, columns, value):
        high, low = split(value)
        ah[rows, columns] = high
        al[rows, columns] = low

    def transposed_split(source):
        dh[...], dl[...] = split(source[...])
        th, tl = split(source[...].T)
        vh[:, 0:W] = th
        vl[:, 0:W] = tl

    half = 256
    transposed_split(d0)

    @pl.loop(0, 2)
    def _(i):
        rows = pl.ds(i * half, half)
        value = dot3((vh[rows, 0:W], vl[rows, 0:W]), (dh[...], dl[...]))
        put(rows, slice(0, W), value)
        cf[rows, :] = value

    q = ((z * 4 + y) * 2 + c) * 4 + x
    eight = cf[pl.ds((q // 2) * 8, 8), :]
    s0[...] = jnp.where(q % 2 == 1, pltpu.roll(eight, 4, 0), eight)

    for level, d, b, c_out, s_out in ((1, d1, b1, c1, s1), (2, d2, b2, c2, s2)):
        k = level * W
        place = (((z * 4 + y) * 2 + c) % (32 >> level)) * 4 + x
        dh[...], dl[...] = split(d[...])

        @pl.loop(0, 2 * level)
        def _(i, b=b):
            rows = pl.ds(i * half, half)
            value = dot3(split(b[rows, :]), (dh[...], dl[...]))
            uh[rows, :], ul[rows, :] = split(value)
            th, tl = split(value.T)
            vh[:, rows] = th
            vl[:, rows] = tl

        @pl.loop(0, 2 * level)
        def _(i, k=k):
            rows = pl.ds(i * half, half)
            value = -dot3((ah[rows, 0:k], al[rows, 0:k]), (uh[0:k, :], ul[0:k, :]))
            cf[rows, :] = value
            ch[rows, :], cl[rows, :] = split(value)
            put(rows, slice(k, k + W), value)
            put(slice(k, k + W), rows, value.T)

        c_out[...] = cf[pl.ds(place * c_out.shape[0], c_out.shape[0]), :]
        cf[0:W, :] = d[...].T

        @pl.loop(0, 2)
        def _(i, k=k):
            rows = pl.ds(i * half, half)
            value = dot3(split(cf[rows, :]), (dh[...], dl[...])) - dot3(
                (vh[rows, 0:k], vl[rows, 0:k]), (ch[0:k, :], cl[0:k, :])
            )
            put(pl.ds(k + i * half, half), slice(k, k + W), value)
            cf[rows, :] = value

        s_out[...] = cf[pl.ds(place * s_out.shape[0], s_out.shape[0]), :]


def upper(parts):
    shapes = [((1536, 1536), BF16)] * 2 + [((8, W), F32), ((8, W), F32), ((8, W), F32), ((32, W), F32), ((16, W), F32)]
    scratch = [pltpu.VMEM((W, W), F32)] * 4 + [pltpu.VMEM((1024, W), F32)]
    scratch += [pltpu.VMEM((W, W), BF16)] * 2 + [pltpu.VMEM((1024, W), BF16)] * 2
    scratch += [pltpu.VMEM((W, 1024), BF16)] * 2 + [pltpu.VMEM((1024, W), BF16)] * 2 + [pltpu.VMEM((1024, W), F32)]
    return pl.pallas_call(
        upper_kernel,
        out_shape=[jax.ShapeDtypeStruct(s, t) for s, t in shapes],
        in_specs=[VMEM] * 10,
        out_specs=[VMEM] * len(shapes),
        scratch_shapes=scratch,
        cost_estimate=pl.CostEstimate(flops=42 * 2 * W**3, bytes_accessed=12 << 20, transcendentals=0),
        name="upper",
    )(*parts)


def lower_kernel(*refs):
    third, fourth, refs = refs[:10], refs[10:20], refs[20:]
    ah, al, c3, s3, own, send = refs[:6]
    d3, d4, bh, bl, b3h, b3l, dh, dl, th, tl, uh, ul, baseh, basel, base, xh, xl, vh, vl, wh, wl, yh, yl = refs[6:]
    z, y, c, x = here()
    for number, (dx, ys) in enumerate([(0, (0, 1)), (1, (0, 1)), (3, (0, 1)), (2, (0,)), (2, (1,))] * 2):
        core = c ^ (number // 5)
        for block, dy in enumerate(ys):
            place = (((y ^ dy) & 1) * 2 + core) * 4 + (x ^ dx)
            source = third[number]
            d3[pl.ds(place * 32, 32), :] = source[block * 128 : block * 128 + 32, :]
            at = pl.ds(place * 96, 96)
            b3h[at, :], b3l[at, :] = split(source[block * 128 + 32 : block * 128 + 128, :])
    for number, (dx, first, last) in enumerate([(0, 0, 320), (1, 0, 320), (3, 0, 320), (2, 0, 160), (2, 160, 320)] * 2):
        place = (c ^ (number // 5)) * 4 + (x ^ dx)
        source = fourth[number]
        if first == 0:
            d4[pl.ds(place * 64, 64), :] = source[0:64, :]
        start = max(first, 64)
        at = pl.ds(place * 256 + start - 64, last - start)
        bh[at, :], bl[at, :] = split(source[start - first : last - first, :])

    half = 256
    dh[...], dl[...] = split(d3[...])
    th[...], tl[...] = split(d3[...].T)

    @pl.loop(0, 2)
    def _(i):
        rows = pl.ds(i * half, half)
        value = dot3((th[rows, :], tl[rows, :]), (dh[...], dl[...]))
        base[rows, :] = value
        baseh[rows, :], basel[rows, :] = split(value)

    @pl.loop(0, 6)
    def _(i):
        rows = pl.ds(i * half, half)
        uh[rows, :], ul[rows, :] = split(dot3((b3h[rows, :], b3l[rows, :]), (dh[...], dl[...])))

    place3 = ((y & 1) * 2 + c) * 4 + x
    piece = pl.ds(place3 * 32, 32)

    @pl.loop(0, 3)
    def _(j):
        rows = pl.ds(j * W, W)
        value = dot3((th[piece, :], tl[piece, :]), (b3h[rows, :], b3l[rows, :]), NT)
        xh[256:288, rows], xl[256:288, rows] = split(value)

    th[...], tl[...] = split(d4[...].T)
    mine = pl.ds(c * half, half)
    one = pl.ds(c * half + x * 64, 64)
    two = pl.ds((1 - c) * half + x * 64, 64)

    @pl.loop(0, 4)
    def _(j):
        rows = pl.ds(j * W, W)
        panel = (bh[rows, :], bl[rows, :])
        vh[0:256, rows], vl[0:256, rows] = split(dot3((th[mine, :], tl[mine, :]), panel, NT))
        vh[256:320, rows], vl[256:320, rows] = split(dot3((th[one, :], tl[one, :]), panel, NT))
        vh[320:384, rows], vl[320:384, rows] = split(dot3((th[two, :], tl[two, :]), panel, NT))

    last = (vh[0:256, 1536:2048], vl[0:256, 1536:2048])

    @pl.loop(0, 3)
    def _(j):
        rows = pl.ds(j * W, W)
        value = vh[0:256, rows].astype(F32) + vl[0:256, rows].astype(F32)
        value = value - dot3((vh[0:256, 1536:2048], vl[0:256, 1536:2048]), (uh[rows, :], ul[rows, :]), NT)
        xh[0:256, rows], xl[0:256, rows] = split(value)

    @pl.loop(0, 3)
    def _(j):
        rows = pl.ds(j * W, W)
        value = -dot3((xh[...], xl[...]), (ah[:, rows], al[:, rows]))
        wh[0:288, rows], wl[0:288, rows] = split(value)

    at = pl.ds(place3 * 96, 96)
    wh[288:384, 0:1536] = ah[at, :]
    wl[288:384, 0:1536] = al[at, :]
    value = dot3((wh[:, 0:1536], wl[:, 0:1536]), (uh[...], ul[...]))
    c3[...] = -value[288:384, :]
    s3[...] = base[piece, :] - value[256:288, :]
    value = -value[0:256, :] - dot3(last, (baseh[...], basel[...]))
    wh[0:256, 1536:2048], wl[0:256, 1536:2048] = split(value)

    for number, (out, core) in enumerate(((own, c), (send, 1 - c))):
        at = pl.ds(core * 1024 + x * 256, 256)
        out[0:256, :] = (wh[0:256, at].astype(F32) + wl[0:256, at].astype(F32)).T
    columns = (wh[0:256, :], wl[0:256, :])
    turned = (th[mine, :], tl[mine, :])
    for out, rows, at in ((own, slice(256, 320), one), (send, slice(320, 384), two)):
        value = dot3((th[at, :], tl[at, :]), turned, NT) - dot3((vh[rows, :], vl[rows, :]), columns, NT)
        out[256:320, :] = value


def lower_levels(third, fourth, ah, al):
    shapes = [((96, W), F32), ((32, W), F32), ((320, 256), F32), ((320, 256), F32)]
    scratch = [pltpu.VMEM((W, W), F32)] * 2 + [pltpu.VMEM((2048, W), BF16)] * 2 + [pltpu.VMEM((1536, W), BF16)] * 2
    scratch += [pltpu.VMEM((W, W), BF16)] * 4 + [pltpu.VMEM((1536, W), BF16)] * 2 + [pltpu.VMEM((W, W), BF16)] * 2
    scratch += [pltpu.VMEM((W, W), F32)] + [pltpu.VMEM((288, 1536), BF16)] * 2 + [pltpu.VMEM((384, 2048), BF16)] * 4
    scratch += [pltpu.VMEM((16, 128), BF16)] * 2
    return pl.pallas_call(
        lower_kernel,
        out_shape=[jax.ShapeDtypeStruct(s, t) for s, t in shapes],
        in_specs=[VMEM] * 22,
        out_specs=[VMEM] * len(shapes),
        scratch_shapes=scratch,
        cost_estimate=pl.CostEstimate(flops=45 * 2 * W**3, bytes_accessed=20 << 20, transcendentals=0),
        name="lower",
    )(*third, *fourth, ah, al)


def finish_kernel(s0, c1, s1, c2, s2, c3, s3, own, got, off, diag):
    c = lax.axis_index("leaf") & 1
    off[...] = jnp.zeros(off.shape, F32)
    diag[...] = jnp.zeros(diag.shape, F32)
    diag[0, 0, 0, 0, 0:8, :] = jnp.where(lax.broadcasted_iota(jnp.int32, (8, W), 0) < 4, s0[...], 0.0)
    for level, c_in, s_in in ((1, c1, s1), (2, c2, s2), (3, c3, s3)):
        off[0, level - 1, 0, 0, 0 : c_in.shape[0], :] = c_in[...]
        diag[0, level, 0, 0, 0 : s_in.shape[0], :] = s_in[...]
    for source, core in ((own, c), (got, 1 - c)):
        columns = pl.ds(core * 256, 256)
        off[0, 3, 0, 0, :, columns] = source[0:256, :]
        diag[0, 4, 0, 0, :, columns] = source[256:320, :]


def finish(pieces, off_shape, diag_shape):
    return pl.pallas_call(
        finish_kernel,
        out_shape=[jax.ShapeDtypeStruct(off_shape, F32), jax.ShapeDtypeStruct(diag_shape, F32)],
        in_specs=[VMEM] * 9,
        out_specs=[VMEM] * 2,
        name="finish",
    )(*pieces)


def on_device(lower, inverse_diag, structure):
    second, top, third, fourth, fifth = pack(structure, lower, inverse_diag)
    one = swap(second, over_z(1))
    two, three = swap(top, over_z(2)), swap(top, over_z(3))
    level3 = swap(fourth, over_y(1))
    early = jnp.concatenate([third, second[:16], one[:16], top[:4], one[16:20], two[:4], three[:4]], 0)
    level4 = both_cores(ring(fifth, over_x))
    early = jnp.concatenate([early] + [swap(early, over_x(bits)) for bits in (1, 2, 3)], 0)
    level3 = both_cores(ring(jnp.concatenate([fourth, level3], 0), over_x))
    early = both_cores(ring(early, over_y))
    ah, al, s0, c1, s1, c2, s2 = upper(early)
    c3, s3, own, send = lower_levels(level3, level4, ah, al)
    got = swap(send, over_core)
    return tuple(finish((s0, c1, s1, c2, s2, c3, s3, own, got), lower.shape, inverse_diag.shape))


def solution(mesh):
    placed = P(None, None, "leaf", "row", None, None)
    return jax.shard_map(
        on_device,
        mesh=mesh,
        in_specs=(placed, placed, P()),
        out_specs=(placed, placed),
        check_vma=False,
    )
```
